32 devices in a mesh: dp: 8 (over z, x), psr: 4 (over y, core).
Axes of the slice: x: 2, y: 2, z: 4, core: 2. Of those that a mesh axis runs over, the one named last changes fastest.
Arguments:
- basis: bfloat16 [32, 4, 8, 128, 256], P(('dp', 'psr')), may hold values from -6 to 6
- residual: bfloat16 [32, 4, 8, 128], P(('dp', 'psr')), may hold values from -6 to 6
- sigma: bfloat16 [32, 4, 8, 128], P(('dp', 'psr')), may hold values from 0.5 to 2
- counts: int32 [32, 4, 8], P(('dp', 'psr')), may hold values from 0 to 128
- pulsar: int32 [32, 4, 8], P(('dp', 'psr')), may hold values from 0 to 3
- ecorr: float32 [16], replicated, may hold values from 0.2 to 2
Outputs:
- gram: float32 [16, 256, 256], P('psr', 'dp')
- rhs: float32 [16, 256], P('psr', 'dp')
- totals: float32 [2], replicated
The draws below stay inside these ranges and needn't reach their ends.
All inputs are finite; a program needn't handle non-finite values.
Results may differ from the reference program's by a relative error of at most 0.0055.
Values may be sent and summed in bfloat16 or wider, within the bound.
A program may use at most 64 MiB of HBM per device.

```python
import math
import jax
import jax.numpy as jnp
from jax import lax

K = 256
L = 128
PG = 4
E_GRP = 8
P_SIZE = 16
SOURCES = 32
NORM_ROWS = 8192
ALL_ROWS = 131072
N_PSR = 4


def plant(entries, stream_key, smallest, top_value):
    index_at = [jax.random.randint(jax.random.fold_in(stream_key, axis), (), 0, length) for axis, length in enumerate(entries.shape)]
    widest = entries.shape.index(max(entries.shape))
    next_to = index_at[:widest] + [(index_at[widest] + 1) % entries.shape[widest]] + index_at[widest + 1:]
    return entries.at[tuple(index_at)].set(smallest).at[tuple(next_to)].set(top_value)


def shard_levels(rng, dims, split, smallest, high):
    def one(axis_at, blocks):
        heights = jax.random.uniform(jax.random.fold_in(jax.random.fold_in(rng, 6), axis_at), (blocks,), jnp.float32, smallest / len(split), high / len(split))
        return jnp.repeat(jnp.exp(heights), dims[axis_at] // blocks).reshape((-1,) + (1,) * (len(dims) - axis_at - 1))

    loudness = one(*split[0])
    for cut in split[1:]:
        loudness = loudness * one(*cut)
    return loudness


def scatter_about(rng, shape, width, reach, shards=(), kind=jnp.bfloat16):
    gain = shard_levels(rng, shape, shards, -0.22, 0.18) if shards else 1.0
    values = jax.random.normal(rng, shape, jnp.float32) * width * gain
    return jnp.minimum(jnp.maximum(values, -reach), reach).astype(kind)


def setup_inputs(seed: int = 0) -> dict:
    seeds = jax.random.split(jax.random.key(seed), 7)
    basis = scatter_about(seeds[0], (SOURCES, N_PSR, E_GRP, L, K), 1.0, 6.0, ((0, 32),))
    residual = scatter_about(seeds[1], (SOURCES, N_PSR, E_GRP, L), 1.0, 6.0, ((0, 32),))
    sigma = jnp.clip(jnp.exp(math.log(2.0) - 1.3862944 * jax.random.uniform(seeds[2], (SOURCES, N_PSR, E_GRP, L), jnp.float32) ** shard_levels(seeds[2], (SOURCES, N_PSR, E_GRP, L), ((0, 32),), -0.2, 0.2)), 0.5, 2.0).astype(jnp.bfloat16)
    counts = plant(jax.random.randint(seeds[3], (SOURCES, N_PSR, E_GRP), 0, L + 1), jax.random.fold_in(seeds[3], 1), 0, L).astype(jnp.int32)
    pulsar = plant(jax.random.randint(seeds[4], (SOURCES, N_PSR, E_GRP), 0, PG), jax.random.fold_in(seeds[4], 1), 0, PG - 1).astype(jnp.int32)
    ecorr = jnp.clip(jnp.exp(jax.random.uniform(seeds[5], (P_SIZE,), jnp.float32, math.log(0.2), math.log(2.0))), 0.2, 2.0)
    return {"basis": basis, "residual": residual, "sigma": sigma, "counts": counts, "pulsar": pulsar, "ecorr": ecorr}


def block_terms(basis, residual, sigma, counts, pulsar, ecorr):
    sig = sigma.astype(jnp.float32)
    res = residual.astype(jnp.float32)
    rowpos = lax.broadcasted_iota(jnp.int32, sig.shape, 2)
    valid = rowpos < counts[..., None]
    inverse = jnp.where(valid, 1.0 / (sig * sig), jnp.float32(0.0))
    weighted = (inverse[..., None] * basis.astype(jnp.float32)).astype(jnp.bfloat16)
    weighted_f = weighted.astype(jnp.float32)
    groups = jnp.arange(N_PSR, dtype=jnp.int32)
    global_id = (groups[:, None] * PG + pulsar).astype(jnp.int32)
    jitter = ecorr[global_id] ** 2
    total = jnp.sum(inverse, axis=2)
    coef = jitter / (1.0 + jitter * total)
    column = jnp.sum(weighted_f, axis=2)
    project = jnp.sum(weighted_f * res[..., None], axis=2)
    wsum = jnp.sum(inverse * res, axis=2)
    chi = jnp.sum(inverse * res * res) - jnp.sum(coef * wsum * wsum)
    logdet = jnp.sum(jnp.where(valid, jnp.log(sig * sig), jnp.float32(0.0))) + jnp.sum(jnp.log(1.0 + jitter * total))
    first = jnp.einsum('gslk,gslm->gskm', basis.astype(jnp.float32), weighted_f, precision=lax.Precision.HIGHEST)
    onehot = (pulsar[..., None] == jnp.arange(PG, dtype=jnp.int32)).astype(jnp.float32)
    gram = jnp.einsum('gsp,gskm->gpkm', onehot, first, precision=lax.Precision.HIGHEST)
    gram = gram - jnp.einsum('gsp,gsk,gsm->gpkm', onehot * coef[..., None], column, column, precision=lax.Precision.HIGHEST)
    rhs = jnp.einsum('gsp,gsk->gpk', onehot, project - (coef * wsum)[..., None] * column, precision=lax.Precision.HIGHEST)
    return gram, rhs, logdet, chi


def reference(basis, residual, sigma, counts, pulsar, ecorr):
    def step(carry, items):
        gram, rhs, logdet, chi = block_terms(items[0], items[1], items[2], items[3], items[4], ecorr)
        return (carry[0] + gram, carry[1] + rhs, carry[2] + logdet, carry[3] + chi), None

    start = (jnp.zeros((N_PSR, PG, K, K), jnp.float32), jnp.zeros((N_PSR, PG, K), jnp.float32), jnp.float32(0.0), jnp.float32(0.0))
    final, _ = lax.scan(step, start, (basis, residual, sigma, counts, pulsar))
    gram = final[0].reshape(P_SIZE, K, K) / NORM_ROWS
    rhs = final[1].reshape(P_SIZE, K) / NORM_ROWS
    totals = jnp.stack([final[2], final[3]]) / ALL_ROWS
    return gram, rhs, totals
```

```python
import functools

import jax
import jax.numpy as jnp
from jax import lax
from jax.experimental import pallas as pl
from jax.experimental.pallas import tpu as pltpu
from jax.sharding import PartitionSpec as P

PG = 4
MESH = pl.DeviceIdType.MESH
F32 = jnp.float32
BF16 = jnp.bfloat16


def column_of(row):
    n = row.shape[1]
    eye = lax.broadcasted_iota(jnp.int32, (n, n), 0) == lax.broadcasted_iota(jnp.int32, (n, n), 1)
    return jnp.sum(jnp.where(eye, jnp.broadcast_to(row, (n, n)), F32(0.0)), axis=1, keepdims=True)


def group_terms(g, basis, res_ref, sig_ref, cnt_ref, pul_ref, ecorr_ref):
    slots, rows, width = basis.shape
    sig = sig_ref[g].astype(F32)
    res = res_ref[g].astype(F32)
    counts = column_of(cnt_ref[pl.ds(g, 1), :].astype(F32))
    pulsar = column_of(pul_ref[pl.ds(g, 1), :].astype(F32))
    lane = lax.broadcasted_iota(jnp.int32, (slots, rows), 1)
    valid = lane.astype(F32) < counts
    var = sig * sig
    inverse = jnp.where(valid, 1.0 / var, F32(0.0))
    total = jnp.sum(inverse, axis=1, keepdims=True)
    n_table = ecorr_ref.shape[1]
    table = lax.broadcasted_iota(jnp.int32, (slots, n_table), 1).astype(F32)
    ids = pulsar + (g * PG).astype(F32)
    chosen = jnp.sum(
        jnp.where(ids == table, jnp.broadcast_to(ecorr_ref[...], (slots, n_table)), F32(0.0)),
        axis=1,
        keepdims=True,
    )
    jitter = chosen * chosen
    coef = jitter / (1.0 + jitter * total)
    wsum = jnp.sum(inverse * res, axis=1, keepdims=True)
    first = lane == 0
    chi = inverse * res * res - jnp.where(first, coef * wsum * wsum, F32(0.0))
    logdet = jnp.where(valid, jnp.log(var), F32(0.0)) + jnp.where(
        first, jnp.log(1.0 + jitter * total), F32(0.0)
    )
    tot = jnp.concatenate(
        [jnp.sum(logdet, axis=0, keepdims=True), jnp.sum(chi, axis=0, keepdims=True)], axis=1
    )

    inv_t = inverse.T
    adj_t = (coef * inverse).T
    blocks = [basis[s] for s in range(slots)]
    weighted = [
        (inv_t[:, s : s + 1] * blocks[s].astype(F32)).astype(BF16) for s in range(slots)
    ]
    member = lax.broadcasted_iota(jnp.int32, (PG, rows), 0).astype(F32)
    onehot = jnp.concatenate(
        [
            jnp.where(member == jnp.broadcast_to(pulsar[s : s + 1], (PG, rows)), F32(1.0), F32(0.0))
            for s in range(slots)
        ],
        axis=1,
    )
    slot = lax.broadcasted_iota(jnp.int32, (slots, rows), 0)
    marks = jnp.concatenate(
        [jnp.where(slot == s, F32(1.0), F32(0.0)) for s in range(slots)], axis=1
    )
    res_row = jnp.concatenate([res[s : s + 1] for s in range(slots)], axis=1)
    left = jnp.concatenate([marks, onehot * res_row, onehot], axis=0).astype(BF16)
    sums = jnp.dot(left, jnp.concatenate(weighted, axis=0), preferred_element_type=F32)
    column = sums[:slots]
    project = sums[slots : slots + PG]
    cw = coef * wsum
    minus = jnp.concatenate(
        [
            jnp.sum(jnp.where(pulsar == F32(m), cw, F32(0.0)) * column, axis=0, keepdims=True)
            for m in range(PG)
        ],
        axis=0,
    )
    rhs = project - minus
    adjusted = jnp.concatenate(
        [
            (weighted[s].astype(F32) - adj_t[:, s : s + 1] * column[s : s + 1]).astype(BF16)
            for s in range(slots)
        ],
        axis=0,
    )
    turned = jnp.concatenate([b.T for b in blocks], axis=1)
    pick = onehot.astype(BF16)

    def gram(m):
        return jnp.dot(turned * pick[m : m + 1], adjusted, preferred_element_type=F32)

    return gram, rhs, tot


def kernel(
    ndp, norm_rows, all_rows,
    basis_ref, res_ref, sig_ref, cnt_ref, pul_ref, ecorr_ref,
    gram_ref, rhs_ref, tot_ref,
    bbuf, out0, in0, out1, in1, own_a, own_b, send_a, send_b,
    in_y, in_xa, in_xb, out_x, in_x, out_y, in_y2, part, out_z, in_z,
    s_core, r_core, s_y, r_y, s_x, r_x, s_z, r_z,
    load_sem, send_sem, recv_sem, zsend_sem, zrecv_sem,
):
    nz = ndp // 2
    half = PG // 2
    dp = lax.axis_index("dp")
    psr = lax.axis_index("psr")
    c, y = psr % 2, psr // 2
    x, z = dp % 2, dp // 2
    c2, y2, x2 = 1 - c, 1 - y, 1 - x
    core_peer = (dp, y * 2 + c2)
    y_peer = (dp, y2 * 2 + c)
    x_peer = (z * 2 + x2, psr)
    order = (y2 * 2 + c2, y2 * 2 + c, y * 2 + c2, psr)

    loads = []
    for i, g in enumerate(order):
        load = pltpu.make_async_copy(basis_ref.at[g], bbuf.at[i], load_sem.at[i])
        load.start()
        loads.append(load)

    z_peers = [(((z + k) % nz) * 2 + x, psr) for k in range(1, nz)]
    barrier = pltpu.get_barrier_semaphore()
    for peer in [core_peer, y_peer, x_peer] + z_peers:
        pl.semaphore_signal(barrier, inc=1, device_id=peer, device_id_type=MESH)

    def send(i, src, dst, peer):
        copy = pltpu.make_async_remote_copy(
            src_ref=src, dst_ref=dst, send_sem=send_sem.at[i], recv_sem=recv_sem.at[i],
            device_id=peer, device_id_type=MESH,
        )
        copy.start()
        return copy

    def shaped(v, ref):
        return v.reshape(ref.shape[1:])

    def terms(i):
        loads[i].wait()
        return group_terms(order[i], bbuf.at[i], res_ref, sig_ref, cnt_ref, pul_ref, ecorr_ref)

    gram, rhs0, tot = terms(0)
    for m in range(PG):
        out0[m] = shaped(gram(m).astype(BF16), out0)
    pl.semaphore_wait(barrier, 2 + nz)
    c0 = send(0, out0, in0, core_peer)

    gram, rhs1, t = terms(1)
    tot = tot + t
    for m in range(PG):
        own_a[m] = shaped(gram(m), own_a)

    gram, rhs2, t = terms(2)
    tot = tot + t
    for m in range(PG):
        out1[m] = shaped(gram(m).astype(BF16), out1)
    c1 = send(1, out1, in1, core_peer)

    c0.wait_recv()
    send_a[...] = (own_a[...] + in0[...].astype(F32)).astype(BF16)
    cy = send(2, send_a.at[pl.ds(0, half)], in_y, y_peer)
    cxa = send(3, send_a.at[pl.ds(half, PG - half), :, x2], in_xa, x_peer)

    gram, rhs3, t = terms(3)
    tot = tot + t
    for m in range(PG):
        own_b[m] = shaped(gram(m), own_b)

    pad = jnp.zeros((3, tot.shape[1]), F32)
    s_core[...] = jnp.concatenate([rhs0, rhs2, tot, pad, jnp.zeros((4, tot.shape[1]), F32)], axis=0)
    cs0 = send(4, s_core, r_core, core_peer)

    c1.wait_recv()
    own_b[...] = own_b[...] + in1[...].astype(F32)
    send_b[...] = own_b[pl.ds(half, PG - half), :, x2].astype(BF16)
    cxb = send(5, send_b, in_xb, x_peer)

    cs0.wait_recv()
    rhs1 = rhs1 + r_core[0:PG]
    rhs3 = rhs3 + r_core[PG : 2 * PG]
    tot = tot + r_core[2 * PG : 2 * PG + 1]
    s_y[...] = jnp.concatenate([rhs1, tot, pad], axis=0)
    cs1 = send(6, s_y, r_y, y_peer)

    cxa.wait_recv()
    out_y[...] = (
        send_a[pl.ds(half, PG - half), :, x].astype(F32) + in_xa[...].astype(F32)
    ).astype(BF16)
    cy2 = send(7, out_y, in_y2, y_peer)

    cy.wait_recv()
    out_x[...] = (own_b[pl.ds(0, half), :, x2] + in_y[:, :, x2].astype(F32)).astype(BF16)
    cx1 = send(8, out_x, in_x, x_peer)
    part[0:half] = own_b[pl.ds(0, half), :, x] + in_y[:, :, x].astype(F32)

    cs1.wait_recv()
    rhs3 = rhs3 + r_y[0:PG]
    tot = tot + r_y[PG : PG + 1]
    s_x[...] = jnp.concatenate([rhs3, tot, pad], axis=0)
    cs2 = send(9, s_x, r_x, x_peer)

    def z_send(h, k, src, dst):
        n = h * (nz - 1) + k - 1
        copy = pltpu.make_async_remote_copy(
            src_ref=src, dst_ref=dst, send_sem=zsend_sem.at[n], recv_sem=zrecv_sem.at[n],
            device_id=z_peers[k - 1], device_id_type=MESH,
        )
        copy.start()
        return copy

    z_copies = []

    def z_stage(h):
        piece = pl.ds(h * half, half)
        for k in range(1, nz):
            zt = (z + k) % nz
            out_z[piece, k - 1] = part[piece, zt].astype(BF16)
            z_copies.append(z_send(h, k, out_z.at[piece, k - 1], in_z.at[piece, k - 1]))

    cxb.wait_recv()
    cy2.wait_recv()
    part[half:PG] = (
        own_b[pl.ds(half, PG - half), :, x] + in_xb[...].astype(F32) + in_y2[...].astype(F32)
    )
    z_stage(1)
    cx1.wait_recv()
    part[0:half] = part[0:half] + in_x[...].astype(F32)
    z_stage(0)

    cs2.wait_recv()
    rhs3 = rhs3 + r_x[0:PG]
    tot = tot + r_x[PG : PG + 1]
    s_z[...] = jnp.concatenate([rhs3, tot, pad], axis=0)
    small = [z_send(2, k, s_z, r_z.at[k - 1]) for k in range(1, nz)]

    for h in (1, 0):
        piece = pl.ds(h * half, half)
        acc = part[piece, z]
        for k in range(1, nz):
            z_copies[(1 - h) * (nz - 1) + k - 1].wait_recv()
            acc = acc + in_z[piece, k - 1].astype(F32)
        gram_ref[piece] = acc / norm_rows

    for k in range(1, nz):
        small[k - 1].wait_recv()
        rhs3 = rhs3 + r_z[k - 1, 0:PG]
        tot = tot + r_z[k - 1, PG : PG + 1]
    share = rhs_ref.shape[1]
    mine = jnp.zeros((PG, share), F32)
    for e in range(ndp):
        mine = mine + jnp.where(dp == e, rhs3[:, e * share : (e + 1) * share], F32(0.0))
    rhs_ref[...] = mine / norm_rows
    rows = tot.shape[1] // 2
    tot_ref[0] = jnp.sum(tot[:, :rows]) / all_rows
    tot_ref[1] = jnp.sum(tot[:, rows:]) / all_rows

    for copy in [c0, c1, cy, cxa, cs0, cxb, cs1, cy2, cx1, cs2] + z_copies + small:
        copy.wait_send()


def fused(basis, residual, sigma, counts, pulsar, ecorr):
    ndp = lax.axis_size("dp")
    groups, slots, rows, width = basis.shape[1:]
    share = width // ndp
    nz = ndp // 2
    half = PG // 2
    norm_rows = float(ndp * slots * rows)
    all_rows = float(ndp * groups * groups * slots * rows)
    vmem = pl.BlockSpec(memory_space=pltpu.VMEM)
    full = (PG, nz, 2, share, width)
    hfull = (half, nz, 2, share, width)
    hpar = (half, nz, share, width)
    n_z = 3 * (nz - 1)
    return pl.pallas_call(
        functools.partial(kernel, ndp, norm_rows, all_rows),
        out_shape=(
            jax.ShapeDtypeStruct((PG, share, width), F32),
            jax.ShapeDtypeStruct((PG, share), F32),
            jax.ShapeDtypeStruct((2,), F32),
        ),
        in_specs=[pl.BlockSpec(memory_space=pl.ANY)] + [vmem] * 5,
        out_specs=(vmem, vmem, pl.BlockSpec(memory_space=pltpu.SMEM)),
        scratch_shapes=[
            pltpu.VMEM((groups, slots, rows, width), BF16),
            pltpu.VMEM(full, BF16),
            pltpu.VMEM(full, BF16),
            pltpu.VMEM(full, BF16),
            pltpu.VMEM(full, BF16),
            pltpu.VMEM(full, F32),
            pltpu.VMEM(full, F32),
            pltpu.VMEM(full, BF16),
            pltpu.VMEM(hpar, BF16),
            pltpu.VMEM(hfull, BF16),
            pltpu.VMEM(hpar, BF16),
            pltpu.VMEM(hpar, BF16),
            pltpu.VMEM(hpar, BF16),
            pltpu.VMEM(hpar, BF16),
            pltpu.VMEM(hpar, BF16),
            pltpu.VMEM(hpar, BF16),
            pltpu.VMEM((PG, nz, share, width), F32),
            pltpu.VMEM((PG, nz - 1, share, width), BF16),
            pltpu.VMEM((PG, nz - 1, share, width), BF16),
            pltpu.VMEM((4 * PG, width), F32),
            pltpu.VMEM((4 * PG, width), F32),
            pltpu.VMEM((2 * PG, width), F32),
            pltpu.VMEM((2 * PG, width), F32),
            pltpu.VMEM((2 * PG, width), F32),
            pltpu.VMEM((2 * PG, width), F32),
            pltpu.VMEM((2 * PG, width), F32),
            pltpu.VMEM((nz - 1, 2 * PG, width), F32),
            pltpu.SemaphoreType.DMA((groups,)),
            pltpu.SemaphoreType.DMA((10,)),
            pltpu.SemaphoreType.DMA((10,)),
            pltpu.SemaphoreType.DMA((n_z,)),
            pltpu.SemaphoreType.DMA((n_z,)),
        ],
        compiler_params=pltpu.CompilerParams(collective_id=0, has_side_effects=True),
    )(basis[0], residual[0], sigma[0], counts[0], pulsar[0], ecorr.reshape(1, -1))


def slot_terms(basis, residual, sigma, counts, pulsar, group_ids, ecorr):
    sig = sigma.astype(jnp.float32)
    res = residual.astype(jnp.float32)
    rowpos = lax.broadcasted_iota(jnp.int32, sig.shape, 2)
    valid = rowpos < counts[..., None]
    inverse = jnp.where(valid, 1.0 / (sig * sig), jnp.float32(0.0))
    weighted = (inverse[..., None] * basis).astype(jnp.bfloat16)
    global_id = group_ids[:, None] * PG + pulsar
    table = jnp.arange(ecorr.shape[0], dtype=jnp.int32)
    chosen = jnp.sum(jnp.where(global_id[..., None] == table, ecorr, jnp.float32(0.0)), axis=-1)
    jitter = chosen * chosen
    total = jnp.sum(inverse, axis=2)
    coef = jitter / (1.0 + jitter * total)
    column = jnp.sum(weighted.astype(jnp.float32), axis=2)
    project = jnp.sum(weighted.astype(jnp.float32) * res[..., None], axis=2)
    wsum = jnp.sum(inverse * res, axis=2)
    chi = jnp.sum(inverse * res * res) - jnp.sum(coef * wsum * wsum)
    logdet = jnp.sum(jnp.where(valid, jnp.log(sig * sig), jnp.float32(0.0))) + jnp.sum(
        jnp.log(1.0 + jitter * total)
    )
    adjusted = project - (coef * wsum)[..., None] * column
    grams = []
    sums = []
    for member in range(PG):
        picked = pulsar == member
        masked = jnp.where(picked[..., None, None], weighted, jnp.zeros((), jnp.bfloat16))
        first = jnp.einsum("gslk,gslm->gkm", basis, masked, preferred_element_type=jnp.float32)
        scale = jnp.where(picked, coef, jnp.float32(0.0))
        minus = jnp.einsum(
            "gs,gsk,gsm->gkm", scale, column, column, precision=lax.Precision.HIGHEST
        )
        grams.append(first - minus)
        sums.append(jnp.sum(jnp.where(picked[..., None], adjusted, jnp.float32(0.0)), axis=1))
    return (jnp.stack(grams, axis=1), jnp.stack(sums, axis=1), logdet, chi)


def on_device(basis, residual, sigma, counts, pulsar, ecorr):
    groups = lax.axis_size("psr")
    ndp = lax.axis_size("dp")
    width = basis.shape[-1]
    rows = basis.shape[-2]
    slots = basis.shape[2]
    share = width // ndp
    group_ids = jnp.arange(groups, dtype=jnp.int32)
    gram, rhs, logdet, chi = slot_terms(
        basis[0], residual[0], sigma[0], counts[0], pulsar[0], group_ids, ecorr
    )
    gram_rows = (
        gram.reshape(groups, PG, ndp, share, width)
        .transpose(2, 0, 1, 3, 4)
        .reshape(ndp * groups * PG * share, width)
    )
    rhs_rows = (
        rhs.reshape(groups, PG, ndp, share).transpose(2, 0, 1, 3).reshape(ndp * groups * PG * share)
    )
    gram_part, rhs_part = (
        lax.psum_scatter(gram_rows, ("dp", "psr"), scatter_dimension=0, tiled=True),
        lax.psum_scatter(rhs_rows, ("dp", "psr"), scatter_dimension=0, tiled=True),
    )
    gram_part = gram_part.reshape(PG, share, width)
    rhs_part = rhs_part.reshape(PG, share)
    summed = lax.psum((logdet, chi), ("dp", "psr"))
    norm_rows = float(ndp * slots * rows)
    all_rows = float(ndp * groups * groups * slots * rows)
    totals = jnp.stack([summed[0], summed[1]]) / all_rows
    return (gram_part / norm_rows, rhs_part / norm_rows, totals)


def solution(mesh):
    def step(basis, *rest):
        groups, _, rows, width = basis.shape[1:]
        ndp = lax.axis_size("dp")
        tiled = ndp % 2 == 0 and ndp > 2 and width % (16 * ndp) == 0 and width == 2 * rows
        if groups == lax.axis_size("psr") == 2 * 2 and tiled:
            return fused(basis, *rest)
        return on_device(basis, *rest)

    return jax.shard_map(
        step,
        mesh=mesh,
        in_specs=(
            P(("dp", "psr"), None, None, None, None),
            P(("dp", "psr"), None, None, None),
            P(("dp", "psr"), None, None, None),
            P(("dp", "psr"), None, None),
            P(("dp", "psr"), None, None),
            P(),
        ),
        out_specs=(P("psr", "dp", None), P("psr", "dp"), P()),
        check_vma=False,
    )
```

```python
import functools

import jax
import jax.numpy as jnp
from jax import lax
from jax.experimental import pallas as pl
from jax.experimental.pallas import tpu as pltpu
from jax.sharding import PartitionSpec as P

PG = 4
MESH = pl.DeviceIdType.MESH
F32 = jnp.float32
BF16 = jnp.bfloat16


def column_of(row):
    n = row.shape[1]
    eye = lax.broadcasted_iota(jnp.int32, (n, n), 0) == lax.broadcasted_iota(jnp.int32, (n, n), 1)
    return jnp.sum(jnp.where(eye, jnp.broadcast_to(row, (n, n)), F32(0.0)), axis=1, keepdims=True)


def group_terms(g, basis, res_ref, sig_ref, cnt_ref, pul_ref, ecorr_ref):
    slots, rows, width = basis.shape
    sig = sig_ref[g].astype(F32)
    res = res_ref[g].astype(F32)
    counts = column_of(cnt_ref[pl.ds(g, 1), :].astype(F32))
    pulsar = column_of(pul_ref[pl.ds(g, 1), :].astype(F32))
    lane = lax.broadcasted_iota(jnp.int32, (slots, rows), 1)
    valid = lane.astype(F32) < counts
    var = sig * sig
    inverse = jnp.where(valid, 1.0 / var, F32(0.0))
    total = jnp.sum(inverse, axis=1, keepdims=True)
    n_table = ecorr_ref.shape[1]
    table = lax.broadcasted_iota(jnp.int32, (slots, n_table), 1).astype(F32)
    ids = pulsar + (g * PG).astype(F32)
    chosen = jnp.sum(
        jnp.where(ids == table, jnp.broadcast_to(ecorr_ref[...], (slots, n_table)), F32(0.0)),
        axis=1,
        keepdims=True,
    )
    jitter = chosen * chosen
    coef = jitter / (1.0 + jitter * total)
    wsum = jnp.sum(inverse * res, axis=1, keepdims=True)
    first = lane == 0
    chi = inverse * res * res - jnp.where(first, coef * wsum * wsum, F32(0.0))
    logdet = jnp.where(valid, jnp.log(var), F32(0.0)) + jnp.where(
        first, jnp.log(1.0 + jitter * total), F32(0.0)
    )
    tot = jnp.concatenate(
        [jnp.sum(logdet, axis=0, keepdims=True), jnp.sum(chi, axis=0, keepdims=True)], axis=1
    )

    inv_t = inverse.T
    adj_t = (coef * inverse).T
    blocks = [basis[s] for s in range(slots)]
    weighted = [
        (inv_t[:, s : s + 1] * blocks[s].astype(F32)).astype(BF16) for s in range(slots)
    ]
    member = lax.broadcasted_iota(jnp.int32, (PG, rows), 0).astype(F32)
    onehot = jnp.concatenate(
        [
            jnp.where(member == jnp.broadcast_to(pulsar[s : s + 1], (PG, rows)), F32(1.0), F32(0.0))
            for s in range(slots)
        ],
        axis=1,
    )
    slot = lax.broadcasted_iota(jnp.int32, (slots, rows), 0)
    marks = jnp.concatenate(
        [jnp.where(slot == s, F32(1.0), F32(0.0)) for s in range(slots)], axis=1
    )
    res_row = jnp.concatenate([res[s : s + 1] for s in range(slots)], axis=1)
    left = jnp.concatenate([marks, onehot * res_row, onehot], axis=0).astype(BF16)
    sums = jnp.dot(left, jnp.concatenate(weighted, axis=0), preferred_element_type=F32)
    column = sums[:slots]
    project = sums[slots : slots + PG]
    cw = coef * wsum
    minus = jnp.concatenate(
        [
            jnp.sum(jnp.where(pulsar == F32(m), cw, F32(0.0)) * column, axis=0, keepdims=True)
            for m in range(PG)
        ],
        axis=0,
    )
    rhs = project - minus
    adjusted = jnp.concatenate(
        [
            (weighted[s].astype(F32) - adj_t[:, s : s + 1] * column[s : s + 1]).astype(BF16)
            for s in range(slots)
        ],
        axis=0,
    )
    turned = jnp.concatenate([b.T for b in blocks], axis=1)
    pick = onehot.astype(BF16)

    def gram(m):
        return jnp.dot(turned * pick[m : m + 1], adjusted, preferred_element_type=F32)

    return gram, rhs, tot


def triangle(n):
    return lax.broadcasted_iota(jnp.int32, (n, n), 0), lax.broadcasted_iota(jnp.int32, (n, n), 1)


def pack(full):
    hw = full.shape[0] // 2
    r, c = triangle(hw)
    low = full[hw:, hw:]
    diag = jnp.sum(jnp.where(r == c, low, F32(0.0)), axis=0, keepdims=True)
    both = jnp.where(r <= c, full[:hw, :hw], low)
    return jnp.concatenate([full[:hw, hw:], both, jnp.broadcast_to(diag, (16, hw))], axis=0)


def unpack(packed):
    hw = packed.shape[1]
    r, c = triangle(hw)
    cross, both = packed[:hw], packed[hw : 2 * hw]
    diag = jnp.broadcast_to(packed[2 * hw : 2 * hw + 1], (hw, hw))
    turned = both.T
    top = jnp.concatenate([jnp.where(r <= c, both, turned), cross], axis=1)
    low = jnp.where(r > c, both, jnp.where(r == c, diag, turned))
    return jnp.concatenate([top, jnp.concatenate([cross.T, low], axis=1)], axis=0)


def kernel(
    ndp,
    basis_ref, res_in, sig_in, cnt_in, pul_in, ecorr_in,
    gram_ref, rhs_ref, tot_ref,
    bbuf, res_ref, sig_ref, cnt_ref, pul_ref, ecorr_ref, out_c, in_c, out_y, in_y, whole, out_x, in_x, out_z, in_z,
    s_core, r_core, s_y, r_y, s_x, r_x, s_z, r_z,
    load_sem, send_sem, recv_sem,
):
    nz = ndp // 2
    dp = lax.axis_index("dp")
    psr = lax.axis_index("psr")
    c, y = psr % 2, psr // 2
    x, z = dp % 2, dp // 2
    c2, y2, x2 = 1 - c, 1 - y, 1 - x
    core_peer = (dp, y * 2 + c2)
    y_peer = (dp, y2 * 2 + c)
    x_peer = (z * 2 + x2, psr)
    order = (y2 * 2 + c2, y2 * 2 + c, y * 2 + c2, psr)

    small_loads = []
    pairs = ((sig_in, sig_ref), (cnt_in, cnt_ref), (res_in, res_ref), (pul_in, pul_ref))
    for i, (src, dst) in enumerate(pairs + ((ecorr_in, ecorr_ref),)):
        load = pltpu.make_async_copy(src, dst, load_sem.at[len(order) + i])
        load.start()
        small_loads.append(load)
    loads = []
    for i, g in enumerate(order):
        load = pltpu.make_async_copy(basis_ref.at[g], bbuf.at[i], load_sem.at[i])
        load.start()
        loads.append(load)

    z_peers = [(((z + k) % nz) * 2 + x, psr) for k in range(1, nz)]
    barrier = pltpu.get_barrier_semaphore()
    for peer in [core_peer, y_peer, x_peer] + z_peers:
        pl.semaphore_signal(barrier, inc=1, device_id=peer, device_id_type=MESH)

    copies = []

    def send(src, dst, peer):
        i = len(copies)
        copy = pltpu.make_async_remote_copy(
            src_ref=src, dst_ref=dst, send_sem=send_sem.at[i], recv_sem=recv_sem.at[i],
            device_id=peer, device_id_type=MESH,
        )
        copy.start()
        copies.append(copy)
        return copy

    def terms(i):
        loads[i].wait()
        return group_terms(order[i], bbuf.at[i], res_ref, sig_ref, cnt_ref, pul_ref, ecorr_ref)

    def core_send(n, value):
        out_c[n] = value.astype(BF16)
        return send(out_c.at[n], in_c.at[n], core_peer)

    for load in small_loads:
        load.wait()
    gram0, rhs0, tot = terms(0)
    first = pack(gram0(0))
    pl.semaphore_wait(barrier, 2 + nz)
    core = [core_send(0, first), core_send(1, pack(gram0(1)))]
    gram1, rhs1, t = terms(1)
    tot = tot + t
    y_copies = []
    for m in range(PG):
        own = pack(gram1(m))
        core[m].wait_recv()
        out_y[m] = (own + in_c[m].astype(F32)).astype(BF16)
        y_copies.append(send(out_y.at[m], in_y.at[m], y_peer))
        if m + 2 < PG:
            core.append(core_send(m + 2, pack(gram0(m + 2))))

    gram2, rhs2, t = terms(2)
    tot = tot + t
    for m in range(PG):
        core.append(core_send(PG + m, pack(gram2(m))))
    gram3, rhs3, t = terms(3)
    tot = tot + t
    pad = jnp.zeros((3, tot.shape[1]), F32)
    s_core[...] = jnp.concatenate([rhs0, rhs2, tot, pad, jnp.zeros((4, tot.shape[1]), F32)], axis=0)
    small_c = send(s_core, r_core, core_peer)

    x_copies = []
    z_copies = []

    def to_x(m):
        own = pack(gram3(m))
        core[PG + m].wait_recv()
        own = own + in_c[PG + m].astype(F32)
        y_copies[m].wait_recv()
        full = unpack(own + in_y[m].astype(F32)).reshape(whole.shape[1:])
        whole[m] = full
        out_x[m] = full.astype(BF16)
        x_copies.append(send(out_x.at[m, :, x2], in_x.at[m], x_peer))

    def to_z(m):
        x_copies[m].wait_recv()
        sent = []
        for k in range(1, nz):
            zt = (z + k) % nz
            out_z[m, k - 1] = (whole[m, zt, x] + in_x[m, zt].astype(F32)).astype(BF16)
            sent.append(send(out_z.at[m, k - 1], in_z.at[m, k - 1], z_peers[k - 1]))
        z_copies.append(sent)

    to_x(0)
    small_c.wait_recv()
    rhs1 = rhs1 + r_core[0:PG]
    rhs3 = rhs3 + r_core[PG : 2 * PG]
    tot = tot + r_core[2 * PG : 2 * PG + 1]
    s_y[...] = jnp.concatenate([rhs1, tot, pad], axis=0)
    small_y = send(s_y, r_y, y_peer)
    to_x(1)
    to_z(0)
    to_x(2)
    to_z(1)
    small_y.wait_recv()
    rhs3 = rhs3 + r_y[0:PG]
    tot = tot + r_y[PG : PG + 1]
    s_x[...] = jnp.concatenate([rhs3, tot, pad], axis=0)
    small_x = send(s_x, r_x, x_peer)
    for m in range(3, PG):
        to_x(m)
        to_z(m - 1)
    small_x.wait_recv()
    rhs3 = rhs3 + r_x[0:PG]
    tot = tot + r_x[PG : PG + 1]
    s_z[...] = jnp.concatenate([rhs3, tot, pad], axis=0)
    small_z = [send(s_z, r_z.at[k - 1], z_peers[k - 1]) for k in range(1, nz)]
    to_z(PG - 1)

    def finish(m):
        acc = whole[m, z, x] + in_x[m, z].astype(F32)
        for k in range(1, nz):
            z_copies[m][k - 1].wait_recv()
            acc = acc + in_z[m, k - 1].astype(F32)
        gram_ref[m] = acc

    for m in range(PG - 1):
        finish(m)
    for k in range(1, nz):
        small_z[k - 1].wait_recv()
        rhs3 = rhs3 + r_z[k - 1, 0:PG]
        tot = tot + r_z[k - 1, PG : PG + 1]
    share = rhs_ref.shape[1]
    mine = jnp.zeros((PG, share), F32)
    for e in range(ndp):
        mine = mine + jnp.where(dp == e, rhs3[:, e * share : (e + 1) * share], F32(0.0))
    rhs_ref[...] = mine
    tot_ref[...] = tot
    finish(PG - 1)
    for copy in copies:
        copy.wait_send()


def scale_kernel(norm_rows, all_rows, gram_in, rhs_in, tot_in, gram_ref, rhs_ref, tot_ref):
    gram_ref[...] = gram_in[...] / norm_rows
    rhs_ref[...] = rhs_in[...] / norm_rows
    rows = tot_in.shape[1] // 2
    tot_ref[0] = jnp.sum(tot_in[:, :rows]) / all_rows
    tot_ref[1] = jnp.sum(tot_in[:, rows:]) / all_rows


def fused(basis, residual, sigma, counts, pulsar, ecorr):
    ndp = lax.axis_size("dp")
    groups, slots, rows, width = basis.shape[1:]
    share = width // ndp
    nz = ndp // 2
    norm_rows = float(ndp * slots * rows)
    all_rows = float(ndp * groups * groups * slots * rows)
    vmem = pl.BlockSpec(memory_space=pltpu.VMEM)
    packed = (width + 16, width // 2)
    n_copies = 4 * PG + (nz - 1) * (PG + 1) + 3
    small = pltpu.VMEM((2 * PG, width), F32)
    sums = pl.pallas_call(
        functools.partial(kernel, ndp),
        out_shape=(
            jax.ShapeDtypeStruct((PG, share, width), F32),
            jax.ShapeDtypeStruct((PG, share), F32),
            jax.ShapeDtypeStruct((1, 2 * rows), F32),
        ),
        in_specs=[pl.BlockSpec(memory_space=pltpu.HBM)] * 6,
        out_specs=(vmem, vmem, vmem),
        scratch_shapes=[
            pltpu.VMEM((groups, slots, rows, width), BF16),
            pltpu.VMEM((groups, slots, rows), BF16),
            pltpu.VMEM((groups, slots, rows), BF16),
            pltpu.VMEM((groups, slots), jnp.int32),
            pltpu.VMEM((groups, slots), jnp.int32),
            pltpu.VMEM((1, ecorr.shape[0]), F32),
            pltpu.VMEM((2 * PG,) + packed, BF16),
            pltpu.VMEM((2 * PG,) + packed, BF16),
            pltpu.VMEM((PG,) + packed, BF16),
            pltpu.VMEM((PG,) + packed, BF16),
            pltpu.VMEM((PG, nz, 2, share, width), F32),
            pltpu.VMEM((PG, nz, 2, share, width), BF16),
            pltpu.VMEM((PG, nz, share, width), BF16),
            pltpu.VMEM((PG, nz - 1, share, width), BF16),
            pltpu.VMEM((PG, nz - 1, share, width), BF16),
            pltpu.VMEM((4 * PG, width), F32),
            pltpu.VMEM((4 * PG, width), F32),
            small, small, small, small, small,
            pltpu.VMEM((nz - 1, 2 * PG, width), F32),
            pltpu.SemaphoreType.DMA((groups + 5,)),
            pltpu.SemaphoreType.DMA((n_copies,)),
            pltpu.SemaphoreType.DMA((n_copies,)),
        ],
        compiler_params=pltpu.CompilerParams(
            collective_id=0, has_side_effects=True
        ),
    )(basis[0], residual[0], sigma[0], counts[0], pulsar[0], ecorr.reshape(1, -1))
    return pl.pallas_call(
        functools.partial(scale_kernel, norm_rows, all_rows),
        out_shape=(
            jax.ShapeDtypeStruct((PG, share, width), F32),
            jax.ShapeDtypeStruct((PG, share), F32),
            jax.ShapeDtypeStruct((2,), F32),
        ),
        in_specs=[vmem] * 3,
        out_specs=(vmem, vmem, pl.BlockSpec(memory_space=pltpu.SMEM)),
    )(*sums)


def slot_terms(basis, residual, sigma, counts, pulsar, group_ids, ecorr):
    sig = sigma.astype(jnp.float32)
    res = residual.astype(jnp.float32)
    rowpos = lax.broadcasted_iota(jnp.int32, sig.shape, 2)
    valid = rowpos < counts[..., None]
    inverse = jnp.where(valid, 1.0 / (sig * sig), jnp.float32(0.0))
    weighted = (inverse[..., None] * basis).astype(jnp.bfloat16)
    global_id = group_ids[:, None] * PG + pulsar
    table = jnp.arange(ecorr.shape[0], dtype=jnp.int32)
    chosen = jnp.sum(jnp.where(global_id[..., None] == table, ecorr, jnp.float32(0.0)), axis=-1)
    jitter = chosen * chosen
    total = jnp.sum(inverse, axis=2)
    coef = jitter / (1.0 + jitter * total)
    column = jnp.sum(weighted.astype(jnp.float32), axis=2)
    project = jnp.sum(weighted.astype(jnp.float32) * res[..., None], axis=2)
    wsum = jnp.sum(inverse * res, axis=2)
    chi = jnp.sum(inverse * res * res) - jnp.sum(coef * wsum * wsum)
    logdet = jnp.sum(jnp.where(valid, jnp.log(sig * sig), jnp.float32(0.0))) + jnp.sum(
        jnp.log(1.0 + jitter * total)
    )
    adjusted = project - (coef * wsum)[..., None] * column
    grams = []
    sums = []
    for member in range(PG):
        picked = pulsar == member
        masked = jnp.where(picked[..., None, None], weighted, jnp.zeros((), jnp.bfloat16))
        first = jnp.einsum("gslk,gslm->gkm", basis, masked, preferred_element_type=jnp.float32)
        scale = jnp.where(picked, coef, jnp.float32(0.0))
        minus = jnp.einsum(
            "gs,gsk,gsm->gkm", scale, column, column, precision=lax.Precision.HIGHEST
        )
        grams.append(first - minus)
        sums.append(jnp.sum(jnp.where(picked[..., None], adjusted, jnp.float32(0.0)), axis=1))
    return (jnp.stack(grams, axis=1), jnp.stack(sums, axis=1), logdet, chi)


def on_device(basis, residual, sigma, counts, pulsar, ecorr):
    groups = lax.axis_size("psr")
    ndp = lax.axis_size("dp")
    width = basis.shape[-1]
    rows = basis.shape[-2]
    slots = basis.shape[2]
    share = width // ndp
    group_ids = jnp.arange(groups, dtype=jnp.int32)
    gram, rhs, logdet, chi = slot_terms(
        basis[0], residual[0], sigma[0], counts[0], pulsar[0], group_ids, ecorr
    )
    gram_rows = (
        gram.reshape(groups, PG, ndp, share, width)
        .transpose(2, 0, 1, 3, 4)
        .reshape(ndp * groups * PG * share, width)
    )
    rhs_rows = (
        rhs.reshape(groups, PG, ndp, share).transpose(2, 0, 1, 3).reshape(ndp * groups * PG * share)
    )
    gram_part, rhs_part = (
        lax.psum_scatter(gram_rows, ("dp", "psr"), scatter_dimension=0, tiled=True),
        lax.psum_scatter(rhs_rows, ("dp", "psr"), scatter_dimension=0, tiled=True),
    )
    gram_part = gram_part.reshape(PG, share, width)
    rhs_part = rhs_part.reshape(PG, share)
    summed = lax.psum((logdet, chi), ("dp", "psr"))
    norm_rows = float(ndp * slots * rows)
    all_rows = float(ndp * groups * groups * slots * rows)
    totals = jnp.stack([summed[0], summed[1]]) / all_rows
    return (gram_part / norm_rows, rhs_part / norm_rows, totals)


def solution(mesh):
    def step(basis, *rest):
        groups, _, rows, width = basis.shape[1:]
        ndp = lax.axis_size("dp")
        tiled = ndp % 2 == 0 and ndp > 2 and width % (16 * ndp) == 0 and width % 256 == 0 and width == 2 * rows
        if groups == lax.axis_size("psr") == 2 * 2 and tiled:
            return fused(basis, *rest)
        return on_device(basis, *rest)

    return jax.shard_map(
        step,
        mesh=mesh,
        in_specs=(
            P(("dp", "psr"), None, None, None, None),
            P(("dp", "psr"), None, None, None),
            P(("dp", "psr"), None, None, None),
            P(("dp", "psr"), None, None),
            P(("dp", "psr"), None, None),
            P(),
        ),
        out_specs=(P("psr", "dp", None), P("psr", "dp"), P()),
        check_vma=False,
    )
```

```python
import functools

import jax
import jax.numpy as jnp
from jax import lax
from jax.experimental import pallas as pl
from jax.experimental.pallas import tpu as pltpu
from jax.sharding import PartitionSpec as P

PG = 4
MESH = pl.DeviceIdType.MESH
F32 = jnp.float32
BF16 = jnp.bfloat16


def column_of(row):
    n = row.shape[1]
    eye = lax.broadcasted_iota(jnp.int32, (n, n), 0) == lax.broadcasted_iota(jnp.int32, (n, n), 1)
    return jnp.sum(jnp.where(eye, jnp.broadcast_to(row, (n, n)), F32(0.0)), axis=1, keepdims=True)


def group_terms(g, basis, res_ref, sig_ref, cnt_ref, pul_ref, ecorr_ref):
    slots, rows, width = basis.shape
    sig = sig_ref[g].astype(F32)
    res = res_ref[g].astype(F32)
    counts = column_of(cnt_ref[pl.ds(g, 1), :].astype(F32))
    pulsar = column_of(pul_ref[pl.ds(g, 1), :].astype(F32))
    lane = lax.broadcasted_iota(jnp.int32, (slots, rows), 1)
    valid = lane.astype(F32) < counts
    var = sig * sig
    inverse = jnp.where(valid, 1.0 / var, F32(0.0))
    total = jnp.sum(inverse, axis=1, keepdims=True)
    n_table = ecorr_ref.shape[1]
    table = lax.broadcasted_iota(jnp.int32, (slots, n_table), 1).astype(F32)
    ids = pulsar + (g * PG).astype(F32)
    chosen = jnp.sum(
        jnp.where(ids == table, jnp.broadcast_to(ecorr_ref[...], (slots, n_table)), F32(0.0)),
        axis=1,
        keepdims=True,
    )
    jitter = chosen * chosen
    coef = jitter / (1.0 + jitter * total)
    wsum = jnp.sum(inverse * res, axis=1, keepdims=True)
    first = lane == 0
    chi = inverse * res * res - jnp.where(first, coef * wsum * wsum, F32(0.0))
    logdet = jnp.where(valid, jnp.log(var), F32(0.0)) + jnp.where(
        first, jnp.log(1.0 + jitter * total), F32(0.0)
    )
    tot = jnp.concatenate(
        [jnp.sum(logdet, axis=0, keepdims=True), jnp.sum(chi, axis=0, keepdims=True)], axis=1
    )

    inv_t = inverse.T
    adj_t = (coef * inverse).T
    blocks = [basis[s] for s in range(slots)]
    weighted = [
        (inv_t[:, s : s + 1] * blocks[s].astype(F32)).astype(BF16) for s in range(slots)
    ]
    member = lax.broadcasted_iota(jnp.int32, (PG, rows), 0).astype(F32)
    onehot = jnp.concatenate(
        [
            jnp.where(member == jnp.broadcast_to(pulsar[s : s + 1], (PG, rows)), F32(1.0), F32(0.0))
            for s in range(slots)
        ],
        axis=1,
    )
    slot = lax.broadcasted_iota(jnp.int32, (slots, rows), 0)
    marks = jnp.concatenate(
        [jnp.where(slot == s, F32(1.0), F32(0.0)) for s in range(slots)], axis=1
    )
    res_row = jnp.concatenate([res[s : s + 1] for s in range(slots)], axis=1)
    left = jnp.concatenate([marks, onehot * res_row, onehot], axis=0).astype(BF16)
    sums = jnp.dot(left, jnp.concatenate(weighted, axis=0), preferred_element_type=F32)
    column = sums[:slots]
    project = sums[slots : slots + PG]
    cw = coef * wsum
    minus = jnp.concatenate(
        [
            jnp.sum(jnp.where(pulsar == F32(m), cw, F32(0.0)) * column, axis=0, keepdims=True)
            for m in range(PG)
        ],
        axis=0,
    )
    rhs = project - minus
    adjusted = jnp.concatenate(
        [
            (weighted[s].astype(F32) - adj_t[:, s : s + 1] * column[s : s + 1]).astype(BF16)
            for s in range(slots)
        ],
        axis=0,
    )
    turned = jnp.concatenate([b.T for b in blocks], axis=1)
    pick = onehot.astype(BF16)

    def gram(m):
        return jnp.dot(turned * pick[m : m + 1], adjusted, preferred_element_type=F32)

    return gram, rhs, tot


def triangle(n):
    return lax.broadcasted_iota(jnp.int32, (n, n), 0), lax.broadcasted_iota(jnp.int32, (n, n), 1)


def pack(full):
    hw = full.shape[0] // 2
    r, c = triangle(hw)
    low = full[hw:, hw:]
    diag = jnp.sum(jnp.where(r == c, low, F32(0.0)), axis=0, keepdims=True)
    both = jnp.where(r <= c, full[:hw, :hw], low)
    return jnp.concatenate([full[:hw, hw:], both, jnp.broadcast_to(diag, (16, hw))], axis=0)


def unpack(packed):
    hw = packed.shape[1]
    r, c = triangle(hw)
    cross, both = packed[:hw], packed[hw : 2 * hw]
    diag = jnp.broadcast_to(packed[2 * hw : 2 * hw + 1], (hw, hw))
    turned = both.T
    top = jnp.concatenate([jnp.where(r <= c, both, turned), cross], axis=1)
    low = jnp.where(r > c, both, jnp.where(r == c, diag, turned))
    return jnp.concatenate([top, jnp.concatenate([cross.T, low], axis=1)], axis=0)


def kernel(
    ndp,
    basis_ref, res_in, sig_in, cnt_in, pul_in, ecorr_in,
    gram_ref, rhs_ref, tot_ref,
    bbuf, res_ref, sig_ref, cnt_ref, pul_ref, ecorr_ref, out_c, in_c, out_y, in_y, whole, out_x, in_x, out_z, in_z,
    s_core, r_core, s_y, r_y, s_x, r_x, s_z, r_z,
    load_sem, send_sem, recv_sem,
):
    nz = ndp // 2
    dp = lax.axis_index("dp")
    psr = lax.axis_index("psr")
    c, y = psr % 2, psr // 2
    x, z = dp % 2, dp // 2
    c2, y2, x2 = 1 - c, 1 - y, 1 - x
    core_peer = (dp, y * 2 + c2)
    y_peer = (dp, y2 * 2 + c)
    x_peer = (z * 2 + x2, psr)
    order = (y2 * 2 + c2, y2 * 2 + c, y * 2 + c2, psr)

    small_loads = []
    pairs = ((sig_in, sig_ref), (cnt_in, cnt_ref), (res_in, res_ref), (pul_in, pul_ref))
    for i, (src, dst) in enumerate(pairs + ((ecorr_in, ecorr_ref),)):
        load = pltpu.make_async_copy(src, dst, load_sem.at[len(order) + i])
        load.start()
        small_loads.append(load)
    loads = []
    for i, g in enumerate(order):
        load = pltpu.make_async_copy(basis_ref.at[g], bbuf.at[i], load_sem.at[i])
        load.start()
        loads.append(load)

    z_peers = [(((z + k) % nz) * 2 + x, psr) for k in range(1, nz)]
    barrier = pltpu.get_barrier_semaphore()
    for peer in [core_peer, y_peer, x_peer] + z_peers:
        pl.semaphore_signal(barrier, inc=1, device_id=peer, device_id_type=MESH)

    copies = []

    def send(src, dst, peer):
        i = len(copies)
        copy = pltpu.make_async_remote_copy(
            src_ref=src, dst_ref=dst, send_sem=send_sem.at[i], recv_sem=recv_sem.at[i],
            device_id=peer, device_id_type=MESH,
        )
        copy.start()
        copies.append(copy)
        return copy

    def terms(i):
        loads[i].wait()
        return group_terms(order[i], bbuf.at[i], res_ref, sig_ref, cnt_ref, pul_ref, ecorr_ref)

    def core_send(n, value):
        out_c[n] = value.astype(BF16)
        return send(out_c.at[n], in_c.at[n], core_peer)

    for load in small_loads:
        load.wait()
    gram0, rhs0, tot = terms(0)
    first = pack(gram0(0))
    pl.semaphore_wait(barrier, 2 + nz)
    core = [core_send(0, first), core_send(1, pack(gram0(1)))]
    gram1, rhs1, t = terms(1)
    tot = tot + t
    y_copies = []
    for m in range(PG):
        own = pack(gram1(m))
        core[m].wait_recv()
        out_y[m] = (own + in_c[m].astype(F32)).astype(BF16)
        y_copies.append(send(out_y.at[m], in_y.at[m], y_peer))
        if m + 2 < PG:
            core.append(core_send(m + 2, pack(gram0(m + 2))))

    gram2, rhs2, t = terms(2)
    tot = tot + t
    gram3, rhs3, t = terms(3)
    tot = tot + t
    pad = jnp.zeros((3, tot.shape[1]), F32)
    s_core[...] = jnp.concatenate([rhs0, rhs2, tot, pad, jnp.zeros((4, tot.shape[1]), F32)], axis=0)
    small_c = send(s_core, r_core, core_peer)

    for m in range(2):
        core.append(core_send(PG + m, pack(gram2(m))))
    x_copies = []
    z_copies = []

    def to_x(m):
        own = pack(gram3(m))
        if m + 2 < PG:
            core.append(core_send(PG + m + 2, pack(gram2(m + 2))))
        core[PG + m].wait_recv()
        own = own + in_c[PG + m].astype(F32)
        y_copies[m].wait_recv()
        full = unpack(own + in_y[m].astype(F32))
        full = full.reshape(nz, 2, *whole.shape[2:])
        out_x[m] = jnp.where(x == 0, full[:, 1], full[:, 0]).astype(BF16)
        x_copies.append(send(out_x.at[m], in_x.at[m], x_peer))
        whole[m] = jnp.where(x == 0, full[:, 0], full[:, 1])

    def to_z(m):
        x_copies[m].wait_recv()
        sent = []
        for k in range(1, nz):
            zt = (z + k) % nz
            out_z[m, k - 1] = (whole[m, zt] + in_x[m, zt].astype(F32)).astype(BF16)
            sent.append(send(out_z.at[m, k - 1], in_z.at[m, k - 1], z_peers[k - 1]))
        z_copies.append(sent)

    to_x(0)
    small_c.wait_recv()
    rhs1 = rhs1 + r_core[0:PG]
    rhs3 = rhs3 + r_core[PG : 2 * PG]
    tot = tot + r_core[2 * PG : 2 * PG + 1]
    s_y[...] = jnp.concatenate([rhs1, tot, pad], axis=0)
    small_y = send(s_y, r_y, y_peer)
    to_x(1)
    to_z(0)
    to_x(2)
    to_z(1)
    small_y.wait_recv()
    rhs3 = rhs3 + r_y[0:PG]
    tot = tot + r_y[PG : PG + 1]
    s_x[...] = jnp.concatenate([rhs3, tot, pad], axis=0)
    small_x = send(s_x, r_x, x_peer)
    for m in range(3, PG):
        to_x(m)
        to_z(m - 1)
    small_x.wait_recv()
    rhs3 = rhs3 + r_x[0:PG]
    tot = tot + r_x[PG : PG + 1]
    s_z[...] = jnp.concatenate([rhs3, tot, pad], axis=0)
    small_z = [send(s_z, r_z.at[k - 1], z_peers[k - 1]) for k in range(1, nz)]
    to_z(PG - 1)

    def finish(m):
        acc = whole[m, z] + in_x[m, z].astype(F32)
        for k in range(1, nz):
            z_copies[m][k - 1].wait_recv()
            acc = acc + in_z[m, k - 1].astype(F32)
        gram_ref[m] = acc

    for m in range(PG - 1):
        finish(m)
    for k in range(1, nz):
        small_z[k - 1].wait_recv()
        rhs3 = rhs3 + r_z[k - 1, 0:PG]
        tot = tot + r_z[k - 1, PG : PG + 1]
    share = rhs_ref.shape[1]
    mine = jnp.zeros((PG, share), F32)
    for e in range(ndp):
        mine = mine + jnp.where(dp == e, rhs3[:, e * share : (e + 1) * share], F32(0.0))
    rhs_ref[...] = mine
    tot_ref[...] = tot
    finish(PG - 1)
    for copy in copies:
        copy.wait_send()


def scale_kernel(norm_rows, all_rows, gram_in, rhs_in, tot_in, gram_ref, rhs_ref, tot_ref):
    gram_ref[...] = gram_in[...] / norm_rows
    rhs_ref[...] = rhs_in[...] / norm_rows
    rows = tot_in.shape[1] // 2
    tot_ref[0] = jnp.sum(tot_in[:, :rows]) / all_rows
    tot_ref[1] = jnp.sum(tot_in[:, rows:]) / all_rows


def fused(basis, residual, sigma, counts, pulsar, ecorr):
    ndp = lax.axis_size("dp")
    groups, slots, rows, width = basis.shape[1:]
    share = width // ndp
    nz = ndp // 2
    norm_rows = float(ndp * slots * rows)
    all_rows = float(ndp * groups * groups * slots * rows)
    vmem = pl.BlockSpec(memory_space=pltpu.VMEM)
    packed = (width + 16, width // 2)
    n_copies = 4 * PG + (nz - 1) * (PG + 1) + 3
    small = pltpu.VMEM((2 * PG, width), F32)
    sums = pl.pallas_call(
        functools.partial(kernel, ndp),
        out_shape=(
            jax.ShapeDtypeStruct((PG, share, width), F32),
            jax.ShapeDtypeStruct((PG, share), F32),
            jax.ShapeDtypeStruct((1, 2 * rows), F32),
        ),
        in_specs=[pl.BlockSpec(memory_space=pltpu.HBM)] * 6,
        out_specs=(vmem, vmem, vmem),
        scratch_shapes=[
            pltpu.VMEM((groups, slots, rows, width), BF16),
            pltpu.VMEM((groups, slots, rows), BF16),
            pltpu.VMEM((groups, slots, rows), BF16),
            pltpu.VMEM((groups, slots), jnp.int32),
            pltpu.VMEM((groups, slots), jnp.int32),
            pltpu.VMEM((1, ecorr.shape[0]), F32),
            pltpu.VMEM((2 * PG,) + packed, BF16),
            pltpu.VMEM((2 * PG,) + packed, BF16),
            pltpu.VMEM((PG,) + packed, BF16),
            pltpu.VMEM((PG,) + packed, BF16),
            pltpu.VMEM((PG, nz, share, width), F32),
            pltpu.VMEM((PG, nz, share, width), BF16),
            pltpu.VMEM((PG, nz, share, width), BF16),
            pltpu.VMEM((PG, nz - 1, share, width), BF16),
            pltpu.VMEM((PG, nz - 1, share, width), BF16),
            pltpu.VMEM((4 * PG, width), F32),
            pltpu.VMEM((4 * PG, width), F32),
            small, small, small, small, small,
            pltpu.VMEM((nz - 1, 2 * PG, width), F32),
            pltpu.SemaphoreType.DMA((groups + 5,)),
            pltpu.SemaphoreType.DMA((n_copies,)),
            pltpu.SemaphoreType.DMA((n_copies,)),
        ],
        compiler_params=pltpu.CompilerParams(
            collective_id=0, has_side_effects=True
        ),
    )(basis[0], residual[0], sigma[0], counts[0], pulsar[0], ecorr.reshape(1, -1))
    return pl.pallas_call(
        functools.partial(scale_kernel, norm_rows, all_rows),
        out_shape=(
            jax.ShapeDtypeStruct((PG, share, width), F32),
            jax.ShapeDtypeStruct((PG, share), F32),
            jax.ShapeDtypeStruct((2,), F32),
        ),
        in_specs=[vmem] * 3,
        out_specs=(vmem, vmem, pl.BlockSpec(memory_space=pltpu.SMEM)),
    )(*sums)


def slot_terms(basis, residual, sigma, counts, pulsar, group_ids, ecorr):
    sig = sigma.astype(jnp.float32)
    res = residual.astype(jnp.float32)
    rowpos = lax.broadcasted_iota(jnp.int32, sig.shape, 2)
    valid = rowpos < counts[..., None]
    inverse = jnp.where(valid, 1.0 / (sig * sig), jnp.float32(0.0))
    weighted = (inverse[..., None] * basis).astype(jnp.bfloat16)
    global_id = group_ids[:, None] * PG + pulsar
    table = jnp.arange(ecorr.shape[0], dtype=jnp.int32)
    chosen = jnp.sum(jnp.where(global_id[..., None] == table, ecorr, jnp.float32(0.0)), axis=-1)
    jitter = chosen * chosen
    total = jnp.sum(inverse, axis=2)
    coef = jitter / (1.0 + jitter * total)
    column = jnp.sum(weighted.astype(jnp.float32), axis=2)
    project = jnp.sum(weighted.astype(jnp.float32) * res[..., None], axis=2)
    wsum = jnp.sum(inverse * res, axis=2)
    chi = jnp.sum(inverse * res * res) - jnp.sum(coef * wsum * wsum)
    logdet = jnp.sum(jnp.where(valid, jnp.log(sig * sig), jnp.float32(0.0))) + jnp.sum(
        jnp.log(1.0 + jitter * total)
    )
    adjusted = project - (coef * wsum)[..., None] * column
    grams = []
    sums = []
    for member in range(PG):
        picked = pulsar == member
        masked = jnp.where(picked[..., None, None], weighted, jnp.zeros((), jnp.bfloat16))
        first = jnp.einsum("gslk,gslm->gkm", basis, masked, preferred_element_type=jnp.float32)
        scale = jnp.where(picked, coef, jnp.float32(0.0))
        minus = jnp.einsum(
            "gs,gsk,gsm->gkm", scale, column, column, precision=lax.Precision.HIGHEST
        )
        grams.append(first - minus)
        sums.append(jnp.sum(jnp.where(picked[..., None], adjusted, jnp.float32(0.0)), axis=1))
    return (jnp.stack(grams, axis=1), jnp.stack(sums, axis=1), logdet, chi)


def on_device(basis, residual, sigma, counts, pulsar, ecorr):
    groups = lax.axis_size("psr")
    ndp = lax.axis_size("dp")
    width = basis.shape[-1]
    rows = basis.shape[-2]
    slots = basis.shape[2]
    share = width // ndp
    group_ids = jnp.arange(groups, dtype=jnp.int32)
    gram, rhs, logdet, chi = slot_terms(
        basis[0], residual[0], sigma[0], counts[0], pulsar[0], group_ids, ecorr
    )
    gram_rows = (
        gram.reshape(groups, PG, ndp, share, width)
        .transpose(2, 0, 1, 3, 4)
        .reshape(ndp * groups * PG * share, width)
    )
    rhs_rows = (
        rhs.reshape(groups, PG, ndp, share).transpose(2, 0, 1, 3).reshape(ndp * groups * PG * share)
    )
    gram_part, rhs_part = (
        lax.psum_scatter(gram_rows, ("dp", "psr"), scatter_dimension=0, tiled=True),
        lax.psum_scatter(rhs_rows, ("dp", "psr"), scatter_dimension=0, tiled=True),
    )
    gram_part = gram_part.reshape(PG, share, width)
    rhs_part = rhs_part.reshape(PG, share)
    summed = lax.psum((logdet, chi), ("dp", "psr"))
    norm_rows = float(ndp * slots * rows)
    all_rows = float(ndp * groups * groups * slots * rows)
    totals = jnp.stack([summed[0], summed[1]]) / all_rows
    return (gram_part / norm_rows, rhs_part / norm_rows, totals)


def solution(mesh):
    def step(basis, *rest):
        groups, _, rows, width = basis.shape[1:]
        ndp = lax.axis_size("dp")
        tiled = ndp % 2 == 0 and ndp > 2 and width % (16 * ndp) == 0 and width % 256 == 0 and width == 2 * rows
        if groups == lax.axis_size("psr") == 2 * 2 and tiled:
            return fused(basis, *rest)
        return on_device(basis, *rest)

    return jax.shard_map(
        step,
        mesh=mesh,
        in_specs=(
            P(("dp", "psr"), None, None, None, None),
            P(("dp", "psr"), None, None, None),
            P(("dp", "psr"), None, None, None),
            P(("dp", "psr"), None, None),
            P(("dp", "psr"), None, None),
            P(),
        ),
        out_specs=(P("psr", "dp", None), P("psr", "dp"), P()),
        check_vma=False,
    )
```
